32 devices in a mesh: groups: 2 (over x), wide: 16 (over z, y, core).
Axes of the slice: x: 2, y: 2, z: 4, core: 2. Of those that a mesh axis runs over, the one named last changes fastest.
Arguments:
- voltages: bfloat16 [512, 265216], P('wide', 'groups'), parts along dimension 1, may hold values from -6 to 6
- antenna_flags: int32 [1024], P(('groups', 'wide')), parts along dimension 0, may hold values 0 or 1
- baseline_pairs: int32 [2, 2048], replicated, may hold values from 0 to 511, as said below
Outputs:
- delay_power: float32 [512, 2048], P('groups', 'wide'), parts along dimension 0
The draws below stay inside these ranges and needn't reach their ends.
There are 2 independent parts, one for each index of `groups`. The reference program is written for one: setup_inputs(seed, part) draws one part's arguments, and reference() takes and returns one part's arrays. A program takes and returns all parts, laid end to end along the dimension named above; an argument that names none is the same for every part. Nothing has to cross between parts.
Inputs may be any that keep to these rules, and one draw needn't show every extreme that they name: `baseline_pairs`: the two inputs of a baseline always differ; baseline 0 pairs input 0 with input 512 - 1.
All inputs are finite; a program needn't handle non-finite values. No bound on the sum of `antenna_flags` on one device may be relied on, other than what follows from the above.
Results may differ from the reference program's by a relative error of at most 0.0055.
Values may be sent and summed in bfloat16 or wider, within the bound.
No kernel may reach another device: no remote copies, remote signals or barrier semaphores. Data moves between devices by JAX's collectives and lax.ppermute only.
A program may use at most 192 MiB of HBM per device.

```python
import math
import jax
import jax.numpy as jnp
from jax import lax

INPUT_COUNT = 512
CHANNEL_COUNT = 256
TAPS = 4
NT = 128
NFFT = 512
SAMPLES = 132608
BASELINE_TOTAL = 2048


def draw_baseline_pairs(key, part):
    leading_key = jax.random.fold_in(key, 11)
    trailing_key = jax.random.fold_in(key, 23)
    first_input = jax.random.randint(leading_key, (BASELINE_TOTAL,), 0, INPUT_COUNT, dtype=jnp.int32)
    start_shift = jax.random.randint(trailing_key, (BASELINE_TOTAL,), 1, INPUT_COUNT, dtype=jnp.int32)
    first_input = first_input.at[0].set(0)
    start_shift = start_shift.at[0].set(INPUT_COUNT - 1)
    second = (first_input + start_shift) % INPUT_COUNT
    return jnp.stack([first_input, second], axis=0).astype(jnp.int32)


def place_ends(array, rng, smallest, largest):
    longest = array.shape.index(max(array.shape))
    spots = []
    for shift in (0, 1):
        where = [jax.random.randint(jax.random.fold_in(rng, axis), (), 0, length) for axis, length in enumerate(array.shape)]
        where[longest] = (where[longest] + shift) % array.shape[longest]
        spots.append(tuple(where))
    return array.at[spots[0]].set(smallest).at[spots[1]].set(largest)


def levels(stream_key, dims, cuts, smallest, top_value):
    level, own = 1.0, jax.random.fold_in(stream_key, 6)
    for axis_at, parts in cuts:
        heights = jnp.exp(jax.random.uniform(jax.random.fold_in(own, axis_at), (parts,), jnp.float32, smallest / len(cuts), top_value / len(cuts)))
        level = level * jnp.repeat(heights, dims[axis_at] // parts).reshape([-1 if axis == axis_at else 1 for axis in range(len(dims))])
    return level


def scatter_about(key, extent, deviation, limit, split=(), kind=jnp.bfloat16):
    entries = jax.random.normal(key, extent, jnp.float32) * deviation
    if len(split) > 0:
        entries = levels(key, extent, split, -0.22, 0.18) * entries
    return jnp.clip(entries, min=-limit, max=limit).astype(kind)


def setup_inputs(seed: int = 0, part: int = 0) -> dict:
    streams_of = jax.random.split(jax.random.key(seed), 4)
    own_keys = jax.random.split(jax.random.fold_in(streams_of[3], part), 4)
    voltages = scatter_about(own_keys[0], (INPUT_COUNT, SAMPLES), 1.0, 6.0, ((0, 16),))
    antenna_flags = place_ends((jax.random.randint(own_keys[1], (INPUT_COUNT,), 0, 8) < 7).astype(jnp.int32), jax.random.fold_in(own_keys[1], 1), 0, 1)
    baseline_pairs = draw_baseline_pairs(jax.random.fold_in(streams_of[3], 71), part)
    return dict(voltages=voltages, antenna_flags=antenna_flags, baseline_pairs=baseline_pairs)


def prototype_table():
    count = TAPS * NFFT
    positions = jnp.arange(count, dtype=jnp.float32)
    start_shift = (positions - count / 2 + 0.5) / NFFT
    hamming = 0.54 - 0.46 * jnp.cos(2 * jnp.pi * positions / (count - 1))
    return (jnp.sinc(start_shift) * hamming).reshape(TAPS, NFFT)

def filter_bank(voltages, antenna_flags, first_input, count):
    framed = voltages.astype(jnp.float32).reshape(voltages.shape[0], -1, NFFT)
    prototype = prototype_table()
    filtered = jnp.zeros((voltages.shape[0], count, NFFT), jnp.float32)
    for tap_index in range(TAPS):
        filtered = filtered + prototype[tap_index][None, None, :] * framed[:, first_input + tap_index:first_input + tap_index + count, :]
    return filtered * antenna_flags.astype(jnp.float32)[:, None, None]

def delay_table():
    chan_int = jnp.arange(CHANNEL_COUNT, dtype=jnp.int32)
    chan_float = chan_int.astype(jnp.float32)
    base = 2 * jnp.pi * chan_float / (CHANNEL_COUNT - 1)
    window = 0.35875 - 0.48829 * jnp.cos(base) + 0.14128 * jnp.cos(2 * base) - 0.01168 * jnp.cos(3 * base)
    phase = chan_int[:, None] * chan_int[None, :] % CHANNEL_COUNT
    angle = 2 * jnp.pi * phase.astype(jnp.float32) / CHANNEL_COUNT
    cosine = jnp.cos(angle) * window[None, :]
    sine = jnp.sin(angle) * window[None, :]
    upper = jnp.concatenate([cosine, sine], axis=1)
    lower = jnp.concatenate([-sine, cosine], axis=1)
    table = jnp.concatenate([upper, lower], axis=0) / jnp.sqrt(jnp.sum(window * window))
    return table.astype(jnp.bfloat16)

def reference(voltages, antenna_flags, baseline_pairs):
    filtered = filter_bank(voltages, antenna_flags, 0, 2 * NT)
    spectrum = jnp.fft.rfft(filtered, axis=-1)[..., :CHANNEL_COUNT] / math.sqrt(NFFT)
    real_part = jnp.real(spectrum).astype(jnp.bfloat16)
    imag_part = jnp.imag(spectrum).astype(jnp.bfloat16)
    by_channel = jnp.transpose(jnp.stack([real_part, imag_part]), (3, 0, 1, 2))
    flat_index = (baseline_pairs[0] * INPUT_COUNT + baseline_pairs[1]).astype(jnp.int32)
    scale = 1.0 / math.sqrt(2 * NT)

    def one_channel(block):
        values = block.astype(jnp.float32)
        total = jnp.zeros((2, INPUT_COUNT, INPUT_COUNT), jnp.float32)
        for batch_index in range(2):
            part = values[:, :, batch_index * NT:(batch_index + 1) * NT]
            swapped = jnp.stack([part[1], -part[0]])
            stacked = jnp.stack([part, swapped])
            total = total + jnp.einsum('qrit,rjt->qij', stacked, part, precision=lax.Precision.HIGHEST)
        picked = total.reshape(2, INPUT_COUNT * INPUT_COUNT)[:, flat_index] * scale
        return picked.astype(jnp.bfloat16)
    cross_visibility = lax.map(one_channel, by_channel)
    column_list = jnp.transpose(cross_visibility, (1, 0, 2)).reshape(2 * CHANNEL_COUNT, BASELINE_TOTAL)
    delays = jnp.dot(delay_table(), column_list, preferred_element_type=jnp.float32)
    return delays[:CHANNEL_COUNT] ** 2 + delays[CHANNEL_COUNT:] ** 2
```

```python
import math

import jax
import jax.numpy as jnp
import numpy as np
from jax import lax
from jax.experimental import pallas as pl
from jax.experimental.pallas import tpu as pltpu
from jax.sharding import PartitionSpec as P

INPUT_COUNT = 512
CHANNEL_COUNT = 256
TAPS = 4
NT = 128
NFFT = 512
HALF = NFFT // 2
FRAMES = 2 * NT

CHUNKS = (96, 128, 32)
BANK_STEP = 8
CORR_STEP = 32
LANES = 128
BASE_TILE = 256


def prototype_np():
    count = TAPS * NFFT
    m = np.arange(count, dtype=np.float64)
    shift = (m - count / 2 + 0.5) / NFFT
    hamming = 0.54 - 0.46 * np.cos(2 * np.pi * m / (count - 1))
    return (np.sinc(shift) * hamming).reshape(TAPS, NFFT).astype(np.float32)


def transform_np(parity, width):
    local = CHANNEL_COUNT // width
    owner = np.arange(width)[:, None, None]
    m = np.arange(local // 2)[None, None, :]
    channel = np.broadcast_to(owner * local + 2 * m + parity, (width, 2, local // 2))
    is_real = np.broadcast_to(np.arange(2)[None, :, None] == 0, channel.shape)
    phase = channel.reshape(-1, 1) * np.arange(HALF)[None, :] % NFFT
    angle = 2 * np.pi * phase / NFFT
    table = np.where(is_real.reshape(-1, 1), np.cos(angle), -np.sin(angle)) / math.sqrt(NFFT)
    high = table.astype(jnp.bfloat16)
    low = (table - high.astype(np.float64)).astype(jnp.bfloat16)
    return np.concatenate([high, high, low], axis=1)


def delay_np(width):
    chan = np.arange(CHANNEL_COUNT)
    base = 2 * np.pi * chan / (CHANNEL_COUNT - 1)
    window = 0.35875 - 0.48829 * np.cos(base) + 0.14128 * np.cos(2 * base) - 0.01168 * np.cos(3 * base)
    angle = 2 * np.pi * (chan[:, None] * chan[None, :] % CHANNEL_COUNT) / CHANNEL_COUNT
    cosine = np.cos(angle) * window[None, :]
    sine = np.sin(angle) * window[None, :]
    upper = np.stack([cosine, sine])
    lower = np.stack([-sine, cosine])
    table = np.concatenate([upper, lower], axis=1) / math.sqrt(np.sum(window * window))
    local = CHANNEL_COUNT // width
    table = table.reshape(2, 2 * CHANNEL_COUNT, width, local // 2, 2).transpose(1, 2, 4, 0, 3)
    return table.reshape(2 * CHANNEL_COUNT, 2 * CHANNEL_COUNT).astype(np.float32).astype(jnp.bfloat16)


def bank_kernel(x_ref, h0_ref, h1_ref, h2_ref, proto_ref, flag_ref, even_ref, odd_ref, y_ref, e_ref, o_ref):
    inputs = x_ref.shape[0]
    rows = 16
    halo = (h0_ref, h1_ref, h2_ref)

    def frame(t, at, column):
        if t < BANK_STEP:
            return x_ref[at : at + rows, t * NFFT + column : t * NFFT + column + LANES].astype(jnp.float32)
        return halo[t - BANK_STEP][at : at + rows, column : column + LANES].astype(jnp.float32)

    for at in range(0, inputs, rows):
        flag = flag_ref[at : at + rows, :]
        for column in range(0, HALF, LANES):
            parts = []
            for side in (column, column + HALF):
                taps = [proto_ref[tap : tap + 1, side : side + LANES] for tap in range(TAPS)]
                window = [frame(t, at, side) for t in range(TAPS - 1)]
                sums = []
                for t in range(BANK_STEP):
                    window.append(frame(t + TAPS - 1, at, side))
                    total = taps[0] * window[0]
                    for tap in range(1, TAPS):
                        total = total + taps[tap] * window[tap]
                    sums.append(total * flag)
                    window.pop(0)
                parts.append(sums)
            for t in range(BANK_STEP):
                first, second = parts[0][t], parts[1][t]
                at_rows = slice(t * inputs + at, t * inputs + at + rows)
                for ref, value in ((e_ref, first + second), (o_ref, first - second)):
                    high = value.astype(jnp.bfloat16)
                    low = (value - high.astype(jnp.float32)).astype(jnp.bfloat16)
                    ref[at_rows, column : column + LANES] = high
                    ref[at_rows, HALF + column : HALF + column + LANES] = low
                    ref[at_rows, 2 * HALF + column : 2 * HALF + column + LANES] = high
    contract = (((1,), (1,)), ((), ()))
    width = y_ref.shape[0]
    part = y_ref.shape[1] // 2
    for parity, (table, data) in enumerate(((even_ref, e_ref), (odd_ref, o_ref))):
        out = lax.dot_general(table[...], data[...], contract, preferred_element_type=jnp.float32)
        out = out.astype(jnp.bfloat16).reshape(width, part, out.shape[1])
        y_ref[:, parity * part : (parity + 1) * part, :] = out


def filter_bank(voltages, proto, flags, even, odd, first, count, width):
    inputs = voltages.shape[0]
    local = CHANNEL_COUNT // width
    step_lanes = BANK_STEP * inputs
    main = pl.BlockSpec((inputs, BANK_STEP * NFFT), lambda j: (0, first // BANK_STEP + j))
    halos = [
        pl.BlockSpec((inputs, NFFT), lambda j, h=h: (0, first + (j + 1) * BANK_STEP + h)) for h in range(TAPS - 1)
    ]
    whole = lambda a: pl.BlockSpec(a.shape, lambda j: (0, 0))
    return pl.pallas_call(
        bank_kernel,
        grid=(count // BANK_STEP,),
        in_specs=[main, *halos, whole(proto), whole(flags), whole(even), whole(odd)],
        out_specs=pl.BlockSpec((width, 2 * local, step_lanes), lambda j: (0, 0, j)),
        out_shape=jax.ShapeDtypeStruct((width, 2 * local, count * inputs), jnp.bfloat16),
        scratch_shapes=[pltpu.VMEM((step_lanes, 3 * HALF), jnp.bfloat16)] * 2,
        compiler_params=pltpu.CompilerParams(vmem_limit_bytes=32 * 2**20),
        cost_estimate=pl.CostEstimate(
            flops=2 * 3 * count * inputs * NFFT * HALF, bytes_accessed=4 * count * inputs * NFFT, transcendentals=0
        ),
        name="bank",
    )(voltages, voltages, voltages, voltages, proto, flags, even, odd)


def corr_kernel(z_ref, first_ref, second_ref, past_ref, out_ref, rows_ref):
    sources, planes, lanes = z_ref.shape
    inputs = INPUT_COUNT // sources
    group = LANES // inputs
    half = planes // 2
    eighth = planes // 4
    frames = lanes // inputs
    step = pl.program_id(0)

    @pl.when(step == 0)
    def _():
        out_ref[...] = past_ref[...]

    for block in range(lanes // LANES):
        for lead in range(0, sources, group):
            tiles = [z_ref[lead + s, :, block * LANES : (block + 1) * LANES] for s in range(group)]
            for t in range(group):
                joined = jnp.concatenate([tile[:, t * inputs : (t + 1) * inputs] for tile in tiles], axis=1)
                at = (block * group + t) * planes
                rows_ref[at : at + planes, lead * inputs : lead * inputs + LANES] = joined

    def tile(k, carry):
        at = pl.ds(pl.multiple_of(k * BASE_TILE, BASE_TILE), BASE_TILE)
        first = jnp.dot(rows_ref[...], first_ref[:, at], preferred_element_type=jnp.float32)
        second = jnp.dot(rows_ref[...], second_ref[:, at], preferred_element_type=jnp.float32)
        first = first.reshape(frames, 2, 2, eighth, BASE_TILE)
        second = second.reshape(frames, 2, 2, eighth, BASE_TILE)
        real = jnp.sum(first[:, :, 0] * second[:, :, 0] + first[:, :, 1] * second[:, :, 1], axis=0)
        imag = jnp.sum(first[:, :, 1] * second[:, :, 0] - first[:, :, 0] * second[:, :, 1], axis=0)
        for parity in range(2):
            base = parity * half
            out_ref[base : base + eighth, at] += real[parity]
            out_ref[base + eighth : base + half, at] += imag[parity]
        return carry

    lax.fori_loop(0, first_ref.shape[1] // BASE_TILE, tile, 0)


def correlate(received, first, second, past):
    sources, planes, lanes = received.shape
    inputs = INPUT_COUNT // sources
    step_lanes = CORR_STEP * inputs
    count = first.shape[1]
    whole = lambda a: pl.BlockSpec(a.shape, lambda j: (0, 0))
    return pl.pallas_call(
        corr_kernel,
        grid=(lanes // step_lanes,),
        in_specs=[
            pl.BlockSpec((sources, planes, step_lanes), lambda j: (0, 0, j)),
            whole(first),
            whole(second),
            whole(past),
        ],
        out_specs=pl.BlockSpec((planes, count), lambda j: (0, 0)),
        out_shape=jax.ShapeDtypeStruct((planes, count), jnp.float32),
        scratch_shapes=[pltpu.VMEM((CORR_STEP * planes, INPUT_COUNT), jnp.bfloat16)],
        compiler_params=pltpu.CompilerParams(vmem_limit_bytes=48 * 2**20),
        cost_estimate=pl.CostEstimate(
            flops=4 * (lanes // inputs) * planes * INPUT_COUNT * count,
            bytes_accessed=2 * sources * planes * lanes + 4 * INPUT_COUNT * count,
            transcendentals=0,
        ),
        name="corr",
    )(received, first, second, past)


def power_kernel(table_ref, values_ref, out_ref):
    delays = jnp.dot(table_ref[...], values_ref[...], preferred_element_type=jnp.float32)
    out_ref[...] = delays[:CHANNEL_COUNT] ** 2 + delays[CHANNEL_COUNT:] ** 2


def delay_power(table, values):
    return pl.pallas_call(
        power_kernel,
        out_shape=jax.ShapeDtypeStruct((CHANNEL_COUNT, values.shape[1]), jnp.float32),
        name="power",
    )(table, values)


def prototype_table():
    count = TAPS * NFFT
    positions = jnp.arange(count, dtype=jnp.float32)
    start_shift = (positions - count / 2 + 0.5) / NFFT
    hamming = 0.54 - 0.46 * jnp.cos(2 * jnp.pi * positions / (count - 1))
    return (jnp.sinc(start_shift) * hamming).reshape(TAPS, NFFT)


def plain_filter_bank(voltages, antenna_flags, first_input, count):
    framed = voltages.astype(jnp.float32).reshape(voltages.shape[0], -1, NFFT)
    prototype = prototype_table()
    filtered = jnp.zeros((voltages.shape[0], count, NFFT), jnp.float32)
    for tap_index in range(TAPS):
        filtered = (
            filtered
            + prototype[tap_index][None, None, :]
            * framed[:, first_input + tap_index : first_input + tap_index + count, :]
        )
    return filtered * antenna_flags.astype(jnp.float32)[:, None, None]


def transform_table():
    rows_int = jnp.arange(2 * CHANNEL_COUNT, dtype=jnp.int32)
    channel = rows_int // 2
    is_real = rows_int % 2 == 0
    sample = jnp.arange(NFFT, dtype=jnp.int32)
    phase = channel[:, None] * sample[None, :] % NFFT
    angle = 2 * jnp.pi * phase.astype(jnp.float32) / NFFT
    table = jnp.where(is_real[:, None], jnp.cos(angle), -jnp.sin(angle))
    return table / math.sqrt(NFFT)


def delay_table():
    chan_int = jnp.arange(CHANNEL_COUNT, dtype=jnp.int32)
    chan_float = chan_int.astype(jnp.float32)
    base = 2 * jnp.pi * chan_float / (CHANNEL_COUNT - 1)
    window = (
        0.35875
        - 0.48829 * jnp.cos(base)
        + 0.14128 * jnp.cos(2 * base)
        - 0.01168 * jnp.cos(3 * base)
    )
    phase = chan_int[:, None] * chan_int[None, :] % CHANNEL_COUNT
    angle = 2 * jnp.pi * phase.astype(jnp.float32) / CHANNEL_COUNT
    cosine = jnp.cos(angle) * window[None, :]
    sine = jnp.sin(angle) * window[None, :]
    upper = jnp.concatenate([cosine, sine], axis=1)
    lower = jnp.concatenate([-sine, cosine], axis=1)
    table = jnp.concatenate([upper, lower], axis=0) / jnp.sqrt(jnp.sum(window * window))
    return table.astype(jnp.bfloat16)


def plain_correlate(received):
    values = received[0]
    swapped = jnp.stack([values[:, 1], -values[:, 0]], axis=1)
    stacked = jnp.stack([values, swapped], axis=0)
    return jnp.einsum("qcrit,crjt->iqcj", stacked, values, preferred_element_type=jnp.float32)


def plain_device(voltages, antenna_flags, baseline_pairs):
    width = lax.axis_size("wide")
    local_inputs = voltages.shape[0]
    local_channels = CHANNEL_COUNT // width
    table = transform_table()
    scale = 1.0 / math.sqrt(2 * NT)
    correlation = jnp.zeros((INPUT_COUNT, 2, local_channels, INPUT_COUNT), jnp.float32)
    for batch_index in range(2):
        filtered = plain_filter_bank(voltages, antenna_flags, batch_index * NT, NT)
        raw = jnp.einsum(
            "kn,itn->kit",
            table,
            filtered,
            precision=lax.Precision.HIGHEST,
            preferred_element_type=jnp.float32,
        )
        correlation = correlation + plain_correlate(
            lax.all_to_all(
                raw.astype(jnp.bfloat16).reshape(width, local_channels, 2, local_inputs, NT),
                "wide",
                split_axis=0,
                concat_axis=3,
                tiled=True,
            )
        )
    baseline_count = baseline_pairs.shape[1]
    block_size = math.gcd(baseline_count, 1024)
    first_blocks = baseline_pairs[0].reshape(baseline_count // block_size, block_size)
    second_blocks = baseline_pairs[1].reshape(baseline_count // block_size, block_size)
    input_positions = jnp.arange(INPUT_COUNT, dtype=jnp.int32)

    def select_block(indices):
        first_block, second_block = indices
        rows_taken = jnp.take(correlation, first_block, axis=0)
        selector = (input_positions[None, :] == second_block[:, None]).astype(jnp.float32)
        return jnp.sum(rows_taken * selector[:, None, None, :], axis=3)

    selected = lax.map(select_block, (first_blocks, second_blocks))
    selected = selected.reshape(baseline_count, 2, local_channels)
    picked = (jnp.transpose(selected, (1, 2, 0)) * scale).astype(jnp.bfloat16)
    regrouped = lax.all_to_all(picked, "wide", split_axis=2, concat_axis=1, tiled=True)
    column_list = regrouped.reshape(2 * CHANNEL_COUNT, regrouped.shape[2])
    delays = jnp.dot(delay_table(), column_list, preferred_element_type=jnp.float32)
    return delays[:CHANNEL_COUNT] ** 2 + delays[CHANNEL_COUNT:] ** 2


def tiles(local_inputs, local_channels, count, width):
    fits = local_inputs % 16 == 0 and LANES % local_inputs == 0 and local_channels % 16 == 0
    return fits and count % BASE_TILE == 0 and (count // width) % LANES == 0


def per_device(voltages, antenna_flags, baseline_pairs):
    width = lax.axis_size("wide")
    local_inputs = voltages.shape[0]
    local_channels = CHANNEL_COUNT // width
    planes = 2 * local_channels
    count = baseline_pairs.shape[1]
    if not tiles(local_inputs, local_channels, count, width):
        return plain_device(voltages, antenna_flags, baseline_pairs)
    proto = jnp.asarray(prototype_np())
    even, odd = (jnp.asarray(transform_np(parity, width)) for parity in range(2))
    flags = antenna_flags.astype(jnp.float32)[:, None]
    inputs = lax.broadcasted_iota(jnp.int32, (INPUT_COUNT, count), 0)
    first = (inputs == baseline_pairs[0][None, :]).astype(jnp.bfloat16)
    second = (inputs == baseline_pairs[1][None, :]).astype(jnp.bfloat16)

    total = jnp.zeros((planes, count), jnp.float32)
    waiting = []
    start = 0
    for frames in CHUNKS:
        spectra = filter_bank(voltages, proto, flags, even, odd, start, frames, width)
        if len(waiting) > 1:
            total = correlate(waiting.pop(0), first, second, total)
            spectra, total = lax.optimization_barrier((spectra, total))
        received = lax.all_to_all(spectra, "wide", split_axis=0, concat_axis=0, tiled=True)
        waiting.append(received)
        start += frames
    for received in waiting:
        total = correlate(received, first, second, total)
    picked = (total * (1.0 / math.sqrt(FRAMES))).astype(jnp.bfloat16)
    picked = picked.reshape(planes, width, count // width).transpose(1, 0, 2)
    regrouped = lax.all_to_all(picked, "wide", split_axis=0, concat_axis=0, tiled=True)
    return delay_power(jnp.asarray(delay_np(width)), regrouped.reshape(2 * CHANNEL_COUNT, count // width))


def solution(mesh):
    placed = (P("wide", "groups"), P(("groups", "wide")), P())
    return jax.shard_map(
        per_device, mesh=mesh, in_specs=placed, out_specs=P("groups", "wide"), check_vma=False
    )
```

```python
import math

import jax
import jax.numpy as jnp
import numpy as np
from jax import lax
from jax.experimental import pallas as pl
from jax.experimental.pallas import tpu as pltpu
from jax.sharding import PartitionSpec as P

INPUT_COUNT = 512
CHANNEL_COUNT = 256
TAPS = 4
NT = 128
NFFT = 512
HALF = NFFT // 2
FRAMES = 2 * NT

CHUNKS = (32, 128, 72, 24)
BANK_STEP = 8
CORR_STEP = 32
GRANT = 58 * 2**20
CORR_GRANT = 32 * 2**20
LANES = 128
BASE_TILE = 256


def prototype_np():
    count = TAPS * NFFT
    m = np.arange(count, dtype=np.float64)
    shift = (m - count / 2 + 0.5) / NFFT
    hamming = 0.54 - 0.46 * np.cos(2 * np.pi * m / (count - 1))
    return (np.sinc(shift) * hamming).reshape(TAPS, NFFT).astype(np.float32)


def transform_np(parity, width):
    local = CHANNEL_COUNT // width
    owner = np.arange(width)[:, None, None]
    m = np.arange(local // 2)[None, None, :]
    channel = np.broadcast_to(owner * local + 2 * m + parity, (width, 2, local // 2))
    is_real = np.broadcast_to(np.arange(2)[None, :, None] == 0, channel.shape)
    phase = channel.reshape(-1, 1) * np.arange(HALF)[None, :] % NFFT
    angle = 2 * np.pi * phase / NFFT
    table = np.where(is_real.reshape(-1, 1), np.cos(angle), -np.sin(angle)) / math.sqrt(NFFT)
    high = table.astype(jnp.bfloat16)
    low = (table - high.astype(np.float64)).astype(jnp.bfloat16)
    return np.concatenate([high, high, low], axis=1)


def delay_np(width):
    chan = np.arange(CHANNEL_COUNT)
    base = 2 * np.pi * chan / (CHANNEL_COUNT - 1)
    window = 0.35875 - 0.48829 * np.cos(base) + 0.14128 * np.cos(2 * base) - 0.01168 * np.cos(3 * base)
    angle = 2 * np.pi * (chan[:, None] * chan[None, :] % CHANNEL_COUNT) / CHANNEL_COUNT
    cosine = np.cos(angle) * window[None, :]
    sine = np.sin(angle) * window[None, :]
    upper = np.stack([cosine, sine])
    lower = np.stack([-sine, cosine])
    table = np.concatenate([upper, lower], axis=1) / math.sqrt(np.sum(window * window))
    local = CHANNEL_COUNT // width
    table = table.reshape(2, 2 * CHANNEL_COUNT, width, local // 2, 2).transpose(1, 2, 4, 0, 3)
    return table.reshape(2 * CHANNEL_COUNT, 2 * CHANNEL_COUNT).astype(np.float32).astype(jnp.bfloat16)


def bank_kernel(x_ref, h0_ref, h1_ref, h2_ref, proto_ref, flag_ref, even_ref, odd_ref, y_ref, e_ref, o_ref):
    inputs = x_ref.shape[0]
    rows = 16
    halo = (h0_ref, h1_ref, h2_ref)

    def frame(t, at, column):
        if t < BANK_STEP:
            return x_ref[at : at + rows, t * NFFT + column : t * NFFT + column + LANES].astype(jnp.float32)
        return halo[t - BANK_STEP][at : at + rows, column : column + LANES].astype(jnp.float32)

    here = lax.broadcasted_iota(jnp.int32, (rows, inputs), 0)
    there = lax.broadcasted_iota(jnp.int32, (rows, inputs), 1)
    for at in range(0, inputs, rows):
        flag = jnp.where(here + at == there, flag_ref[...].astype(jnp.float32), 0.0)
        flag = jnp.sum(flag, axis=1, keepdims=True)
        for column in range(0, HALF, LANES):
            parts = []
            for side in (column, column + HALF):
                taps = [proto_ref[tap : tap + 1, side : side + LANES] for tap in range(TAPS)]
                window = [frame(t, at, side) for t in range(TAPS - 1)]
                sums = []
                for t in range(BANK_STEP):
                    window.append(frame(t + TAPS - 1, at, side))
                    total = taps[0] * window[0]
                    for tap in range(1, TAPS):
                        total = total + taps[tap] * window[tap]
                    sums.append(total * flag)
                    window.pop(0)
                parts.append(sums)
            for t in range(BANK_STEP):
                first, second = parts[0][t], parts[1][t]
                at_rows = slice(t * inputs + at, t * inputs + at + rows)
                for ref, value in ((e_ref, first + second), (o_ref, first - second)):
                    high = value.astype(jnp.bfloat16)
                    low = (value - high.astype(jnp.float32)).astype(jnp.bfloat16)
                    ref[at_rows, column : column + LANES] = high
                    ref[at_rows, HALF + column : HALF + column + LANES] = low
                    ref[at_rows, 2 * HALF + column : 2 * HALF + column + LANES] = high
    contract = (((1,), (1,)), ((), ()))
    width = y_ref.shape[0]
    part = y_ref.shape[1] // 2
    for parity, (table, data) in enumerate(((even_ref, e_ref), (odd_ref, o_ref))):
        out = lax.dot_general(table[...], data[...], contract, preferred_element_type=jnp.float32)
        out = out.astype(jnp.bfloat16).reshape(width, part, out.shape[1])
        y_ref[:, parity * part : (parity + 1) * part, :] = out


def filter_bank(voltages, proto, flags, even, odd, first, count, width):
    inputs = voltages.shape[0]
    local = CHANNEL_COUNT // width
    step_lanes = BANK_STEP * inputs
    main = pl.BlockSpec((inputs, BANK_STEP * NFFT), lambda j: (0, first // BANK_STEP + j))
    halos = [
        pl.BlockSpec((inputs, NFFT), lambda j, h=h: (0, first + (j + 1) * BANK_STEP + h)) for h in range(TAPS - 1)
    ]
    whole = lambda a: pl.BlockSpec(a.shape, lambda j: (0, 0))
    return pl.pallas_call(
        bank_kernel,
        grid=(count // BANK_STEP,),
        in_specs=[main, *halos, whole(proto), whole(flags), whole(even), whole(odd)],
        out_specs=pl.BlockSpec((width, 2 * local, step_lanes), lambda j: (0, 0, j)),
        out_shape=jax.ShapeDtypeStruct((width, 2 * local, count * inputs), jnp.bfloat16),
        scratch_shapes=[pltpu.VMEM((step_lanes, 3 * HALF), jnp.bfloat16)] * 2,
        compiler_params=pltpu.CompilerParams(vmem_limit_bytes=GRANT),
        cost_estimate=pl.CostEstimate(
            flops=2 * 3 * count * inputs * NFFT * HALF, bytes_accessed=4 * count * inputs * NFFT, transcendentals=0
        ),
        name="bank",
    )(voltages, voltages, voltages, voltages, proto, flags, even, odd)


def corr_kernel(z_ref, pairs_ref, past_ref, out_ref, rows_ref, first_ref, second_ref):
    sources, planes, lanes = z_ref.shape
    inputs = INPUT_COUNT // sources
    group = LANES // inputs
    half = planes // 2
    eighth = planes // 4
    frames = lanes // inputs
    step = pl.program_id(0)

    @pl.when(step == 0)
    def _():
        out_ref[...] = past_ref[...]
        index = lax.broadcasted_iota(jnp.int32, (INPUT_COUNT, BASE_TILE), 0)

        def select(k, carry):
            at = pl.ds(pl.multiple_of(k * BASE_TILE, BASE_TILE), BASE_TILE)
            for row, ref in enumerate((first_ref, second_ref)):
                hit = index == pairs_ref[row : row + 1, at]
                ref[:, at] = jnp.where(hit, 1.0, 0.0).astype(jnp.bfloat16)
            return carry

        lax.fori_loop(0, pairs_ref.shape[1] // BASE_TILE, select, 0)

    for block in range(lanes // LANES):
        for lead in range(0, sources, group):
            tiles = [z_ref[lead + s, :, block * LANES : (block + 1) * LANES] for s in range(group)]
            for t in range(group):
                joined = jnp.concatenate([tile[:, t * inputs : (t + 1) * inputs] for tile in tiles], axis=1)
                at = (block * group + t) * planes
                rows_ref[at : at + planes, lead * inputs : lead * inputs + LANES] = joined

    def tile(k, carry):
        at = pl.ds(pl.multiple_of(k * BASE_TILE, BASE_TILE), BASE_TILE)
        first = jnp.dot(rows_ref[...], first_ref[:, at], preferred_element_type=jnp.float32)
        second = jnp.dot(rows_ref[...], second_ref[:, at], preferred_element_type=jnp.float32)
        first = first.reshape(frames, 2, 2, eighth, BASE_TILE)
        second = second.reshape(frames, 2, 2, eighth, BASE_TILE)
        real = jnp.sum(first[:, :, 0] * second[:, :, 0] + first[:, :, 1] * second[:, :, 1], axis=0)
        imag = jnp.sum(first[:, :, 1] * second[:, :, 0] - first[:, :, 0] * second[:, :, 1], axis=0)
        for parity in range(2):
            base = parity * half
            out_ref[base : base + eighth, at] += real[parity]
            out_ref[base + eighth : base + half, at] += imag[parity]
        return carry

    lax.fori_loop(0, first_ref.shape[1] // BASE_TILE, tile, 0)


def correlate(received, pairs, past):
    sources, planes, lanes = received.shape
    inputs = INPUT_COUNT // sources
    frames = lanes // inputs
    per_step = max(f for f in range(BANK_STEP, CORR_STEP + 1, BANK_STEP) if frames % f == 0)
    count = pairs.shape[1]
    whole = lambda a: pl.BlockSpec(a.shape, lambda j: (0, 0))
    return pl.pallas_call(
        corr_kernel,
        grid=(frames // per_step,),
        in_specs=[
            pl.BlockSpec((sources, planes, per_step * inputs), lambda j: (0, 0, j)),
            whole(pairs),
            whole(past),
        ],
        out_specs=pl.BlockSpec((planes, count), lambda j: (0, 0)),
        out_shape=jax.ShapeDtypeStruct((planes, count), jnp.float32),
        scratch_shapes=[
            pltpu.VMEM((per_step * planes, INPUT_COUNT), jnp.bfloat16),
            pltpu.VMEM((INPUT_COUNT, count), jnp.bfloat16),
            pltpu.VMEM((INPUT_COUNT, count), jnp.bfloat16),
        ],
        compiler_params=pltpu.CompilerParams(vmem_limit_bytes=CORR_GRANT),
        cost_estimate=pl.CostEstimate(
            flops=4 * frames * planes * INPUT_COUNT * count,
            bytes_accessed=2 * sources * planes * lanes,
            transcendentals=0,
        ),
        name="corr",
    )(received, pairs, past)


def power_kernel(table_ref, values_ref, out_ref):
    delays = jnp.dot(table_ref[...], values_ref[...], preferred_element_type=jnp.float32)
    out_ref[...] = delays[:CHANNEL_COUNT] ** 2 + delays[CHANNEL_COUNT:] ** 2


def delay_power(table, values):
    return pl.pallas_call(
        power_kernel,
        out_shape=jax.ShapeDtypeStruct((CHANNEL_COUNT, values.shape[1]), jnp.float32),
        name="power",
    )(table, values)


def prototype_table():
    count = TAPS * NFFT
    positions = jnp.arange(count, dtype=jnp.float32)
    start_shift = (positions - count / 2 + 0.5) / NFFT
    hamming = 0.54 - 0.46 * jnp.cos(2 * jnp.pi * positions / (count - 1))
    return (jnp.sinc(start_shift) * hamming).reshape(TAPS, NFFT)


def plain_filter_bank(voltages, antenna_flags, first_input, count):
    framed = voltages.astype(jnp.float32).reshape(voltages.shape[0], -1, NFFT)
    prototype = prototype_table()
    filtered = jnp.zeros((voltages.shape[0], count, NFFT), jnp.float32)
    for tap_index in range(TAPS):
        filtered = (
            filtered
            + prototype[tap_index][None, None, :]
            * framed[:, first_input + tap_index : first_input + tap_index + count, :]
        )
    return filtered * antenna_flags.astype(jnp.float32)[:, None, None]


def transform_table():
    rows_int = jnp.arange(2 * CHANNEL_COUNT, dtype=jnp.int32)
    channel = rows_int // 2
    is_real = rows_int % 2 == 0
    sample = jnp.arange(NFFT, dtype=jnp.int32)
    phase = channel[:, None] * sample[None, :] % NFFT
    angle = 2 * jnp.pi * phase.astype(jnp.float32) / NFFT
    table = jnp.where(is_real[:, None], jnp.cos(angle), -jnp.sin(angle))
    return table / math.sqrt(NFFT)


def delay_table():
    chan_int = jnp.arange(CHANNEL_COUNT, dtype=jnp.int32)
    chan_float = chan_int.astype(jnp.float32)
    base = 2 * jnp.pi * chan_float / (CHANNEL_COUNT - 1)
    window = (
        0.35875
        - 0.48829 * jnp.cos(base)
        + 0.14128 * jnp.cos(2 * base)
        - 0.01168 * jnp.cos(3 * base)
    )
    phase = chan_int[:, None] * chan_int[None, :] % CHANNEL_COUNT
    angle = 2 * jnp.pi * phase.astype(jnp.float32) / CHANNEL_COUNT
    cosine = jnp.cos(angle) * window[None, :]
    sine = jnp.sin(angle) * window[None, :]
    upper = jnp.concatenate([cosine, sine], axis=1)
    lower = jnp.concatenate([-sine, cosine], axis=1)
    table = jnp.concatenate([upper, lower], axis=0) / jnp.sqrt(jnp.sum(window * window))
    return table.astype(jnp.bfloat16)


def plain_correlate(received):
    values = received[0]
    swapped = jnp.stack([values[:, 1], -values[:, 0]], axis=1)
    stacked = jnp.stack([values, swapped], axis=0)
    return jnp.einsum("qcrit,crjt->iqcj", stacked, values, preferred_element_type=jnp.float32)


def plain_device(voltages, antenna_flags, baseline_pairs):
    width = lax.axis_size("wide")
    local_inputs = voltages.shape[0]
    local_channels = CHANNEL_COUNT // width
    table = transform_table()
    scale = 1.0 / math.sqrt(2 * NT)
    correlation = jnp.zeros((INPUT_COUNT, 2, local_channels, INPUT_COUNT), jnp.float32)
    for batch_index in range(2):
        filtered = plain_filter_bank(voltages, antenna_flags, batch_index * NT, NT)
        raw = jnp.einsum(
            "kn,itn->kit",
            table,
            filtered,
            precision=lax.Precision.HIGHEST,
            preferred_element_type=jnp.float32,
        )
        correlation = correlation + plain_correlate(
            lax.all_to_all(
                raw.astype(jnp.bfloat16).reshape(width, local_channels, 2, local_inputs, NT),
                "wide",
                split_axis=0,
                concat_axis=3,
                tiled=True,
            )
        )
    baseline_count = baseline_pairs.shape[1]
    block_size = math.gcd(baseline_count, 1024)
    first_blocks = baseline_pairs[0].reshape(baseline_count // block_size, block_size)
    second_blocks = baseline_pairs[1].reshape(baseline_count // block_size, block_size)
    input_positions = jnp.arange(INPUT_COUNT, dtype=jnp.int32)

    def select_block(indices):
        first_block, second_block = indices
        rows_taken = jnp.take(correlation, first_block, axis=0)
        selector = (input_positions[None, :] == second_block[:, None]).astype(jnp.float32)
        return jnp.sum(rows_taken * selector[:, None, None, :], axis=3)

    selected = lax.map(select_block, (first_blocks, second_blocks))
    selected = selected.reshape(baseline_count, 2, local_channels)
    picked = (jnp.transpose(selected, (1, 2, 0)) * scale).astype(jnp.bfloat16)
    regrouped = lax.all_to_all(picked, "wide", split_axis=2, concat_axis=1, tiled=True)
    column_list = regrouped.reshape(2 * CHANNEL_COUNT, regrouped.shape[2])
    delays = jnp.dot(delay_table(), column_list, preferred_element_type=jnp.float32)
    return delays[:CHANNEL_COUNT] ** 2 + delays[CHANNEL_COUNT:] ** 2


def tiles(local_inputs, local_channels, count, width):
    fits = local_inputs % 16 == 0 and LANES % local_inputs == 0 and local_channels % 16 == 0
    return fits and count % BASE_TILE == 0 and (count // width) % LANES == 0


def per_device(voltages, antenna_flags, baseline_pairs):
    width = lax.axis_size("wide")
    local_inputs = voltages.shape[0]
    local_channels = CHANNEL_COUNT // width
    planes = 2 * local_channels
    count = baseline_pairs.shape[1]
    if not tiles(local_inputs, local_channels, count, width):
        return plain_device(voltages, antenna_flags, baseline_pairs)
    proto = jnp.asarray(prototype_np())
    even, odd = (jnp.asarray(transform_np(parity, width)) for parity in range(2))
    flags = antenna_flags[None, :]

    total = jnp.zeros((planes, count), jnp.float32)
    waiting = []
    start = 0
    for frames in CHUNKS:
        spectra = filter_bank(voltages, proto, flags, even, odd, start, frames, width)
        if len(waiting) > 1:
            total = correlate(waiting.pop(0), baseline_pairs, total)
            spectra, total = lax.optimization_barrier((spectra, total))
        received = lax.all_to_all(spectra, "wide", split_axis=0, concat_axis=0, tiled=True)
        waiting.append(received)
        start += frames
    for received in waiting:
        total = correlate(received, baseline_pairs, total)
    picked = (total * (1.0 / math.sqrt(FRAMES))).astype(jnp.bfloat16)
    picked = picked.reshape(planes, width, count // width).transpose(1, 0, 2)
    regrouped = lax.all_to_all(picked, "wide", split_axis=0, concat_axis=0, tiled=True)
    return delay_power(jnp.asarray(delay_np(width)), regrouped.reshape(2 * CHANNEL_COUNT, count // width))


def solution(mesh):
    placed = (P("wide", "groups"), P(("groups", "wide")), P())
    return jax.shard_map(
        per_device, mesh=mesh, in_specs=placed, out_specs=P("groups", "wide"), check_vma=False
    )
```

```python
import math

import jax
import jax.numpy as jnp
import numpy as np
from jax import lax
from jax.experimental import pallas as pl
from jax.experimental.pallas import tpu as pltpu
from jax.sharding import PartitionSpec as P

INPUT_COUNT = 512
CHANNEL_COUNT = 256
TAPS = 4
NT = 128
NFFT = 512
HALF = NFFT // 2
FRAMES = 2 * NT

CHUNKS = (32, 144, 56, 24)
BANK_STEP = 8
CORR_STEP = 32
BANK_GRANT = 58 * 2**20
CORR_GRANT = 28 * 2**20
POWER_GRANT = 8 * 2**20
LANES = 128
BASE_TILE = 256
UNROLL = 2


def prototype_np():
    count = TAPS * NFFT
    m = np.arange(count, dtype=np.float64)
    shift = (m - count / 2 + 0.5) / NFFT
    hamming = 0.54 - 0.46 * np.cos(2 * np.pi * m / (count - 1))
    return (np.sinc(shift) * hamming).reshape(TAPS, NFFT).astype(np.float32)


def transform_np(parity, width):
    local = CHANNEL_COUNT // width
    owner = np.arange(width)[:, None, None]
    m = np.arange(local // 2)[None, None, :]
    channel = np.broadcast_to(owner * local + 2 * m + parity, (width, 2, local // 2))
    is_real = np.broadcast_to(np.arange(2)[None, :, None] == 0, channel.shape)
    phase = channel.reshape(-1, 1) * np.arange(HALF)[None, :] % NFFT
    angle = 2 * np.pi * phase / NFFT
    table = np.where(is_real.reshape(-1, 1), np.cos(angle), -np.sin(angle)) / math.sqrt(NFFT)
    high = table.astype(jnp.bfloat16)
    low = (table - high.astype(np.float64)).astype(jnp.bfloat16)
    return np.concatenate([high, high, low], axis=1)


def delay_np(width):
    chan = np.arange(CHANNEL_COUNT)
    base = 2 * np.pi * chan / (CHANNEL_COUNT - 1)
    window = 0.35875 - 0.48829 * np.cos(base) + 0.14128 * np.cos(2 * base) - 0.01168 * np.cos(3 * base)
    angle = 2 * np.pi * (chan[:, None] * chan[None, :] % CHANNEL_COUNT) / CHANNEL_COUNT
    cosine = np.cos(angle) * window[None, :]
    sine = np.sin(angle) * window[None, :]
    upper = np.stack([cosine, sine])
    lower = np.stack([-sine, cosine])
    table = np.concatenate([upper, lower], axis=1) / math.sqrt(np.sum(window * window))
    local = CHANNEL_COUNT // width
    table = table.reshape(2, 2 * CHANNEL_COUNT, width, local // 2, 2).transpose(1, 2, 4, 0, 3)
    return table.reshape(2 * CHANNEL_COUNT, 2 * CHANNEL_COUNT).astype(np.float32).astype(jnp.bfloat16)


def bank_kernel(x_ref, h0_ref, h1_ref, h2_ref, proto_ref, flag_ref, even_ref, odd_ref, y_ref, e_ref, o_ref):
    inputs = x_ref.shape[0]
    rows = 16
    halo = (h0_ref, h1_ref, h2_ref)

    def frame(t, at, column):
        if t < BANK_STEP:
            return x_ref[at : at + rows, t * NFFT + column : t * NFFT + column + LANES].astype(jnp.float32)
        return halo[t - BANK_STEP][at : at + rows, column : column + LANES].astype(jnp.float32)

    here = lax.broadcasted_iota(jnp.int32, (rows, inputs), 0)
    there = lax.broadcasted_iota(jnp.int32, (rows, inputs), 1)
    for at in range(0, inputs, rows):
        flag = jnp.where(here + at == there, flag_ref[...].astype(jnp.float32), 0.0)
        flag = jnp.sum(flag, axis=1, keepdims=True)
        for column in range(0, HALF, LANES):
            parts = []
            for side in (column, column + HALF):
                taps = [proto_ref[tap : tap + 1, side : side + LANES] for tap in range(TAPS)]
                window = [frame(t, at, side) for t in range(TAPS - 1)]
                sums = []
                for t in range(BANK_STEP):
                    window.append(frame(t + TAPS - 1, at, side))
                    total = taps[0] * window[0]
                    for tap in range(1, TAPS):
                        total = total + taps[tap] * window[tap]
                    sums.append(total * flag)
                    window.pop(0)
                parts.append(sums)
            for t in range(BANK_STEP):
                first, second = parts[0][t], parts[1][t]
                at_rows = slice(t * inputs + at, t * inputs + at + rows)
                for ref, value in ((e_ref, first + second), (o_ref, first - second)):
                    high = value.astype(jnp.bfloat16)
                    low = (value - high.astype(jnp.float32)).astype(jnp.bfloat16)
                    ref[at_rows, column : column + LANES] = high
                    ref[at_rows, HALF + column : HALF + column + LANES] = low
                    ref[at_rows, 2 * HALF + column : 2 * HALF + column + LANES] = high
    contract = (((1,), (1,)), ((), ()))
    width = y_ref.shape[0]
    part = y_ref.shape[1] // 2
    for parity, (table, data) in enumerate(((even_ref, e_ref), (odd_ref, o_ref))):
        out = lax.dot_general(table[...], data[...], contract, preferred_element_type=jnp.float32)
        out = out.astype(jnp.bfloat16).reshape(width, part, out.shape[1])
        y_ref[:, parity * part : (parity + 1) * part, :] = out


def filter_bank(voltages, proto, flags, even, odd, first, count, width):
    inputs = voltages.shape[0]
    local = CHANNEL_COUNT // width
    step_lanes = BANK_STEP * inputs
    main = pl.BlockSpec((inputs, BANK_STEP * NFFT), lambda j: (0, first // BANK_STEP + j))
    halos = [
        pl.BlockSpec((inputs, NFFT), lambda j, h=h: (0, first + (j + 1) * BANK_STEP + h)) for h in range(TAPS - 1)
    ]
    whole = lambda a: pl.BlockSpec(a.shape, lambda j: (0, 0))
    return pl.pallas_call(
        bank_kernel,
        grid=(count // BANK_STEP,),
        in_specs=[main, *halos, whole(proto), whole(flags), whole(even), whole(odd)],
        out_specs=pl.BlockSpec((width, 2 * local, step_lanes), lambda j: (0, 0, j)),
        out_shape=jax.ShapeDtypeStruct((width, 2 * local, count * inputs), jnp.bfloat16),
        scratch_shapes=[pltpu.VMEM((step_lanes, 3 * HALF), jnp.bfloat16)] * 2,
        compiler_params=pltpu.CompilerParams(vmem_limit_bytes=BANK_GRANT),
        cost_estimate=pl.CostEstimate(
            flops=2 * 3 * count * inputs * NFFT * HALF, bytes_accessed=4 * count * inputs * NFFT, transcendentals=0
        ),
        name="bank",
    )(voltages, voltages, voltages, voltages, proto, flags, even, odd)


def corr_kernel(z_ref, pairs_ref, past_ref, out_ref, rows_ref):
    sources, planes, lanes = z_ref.shape
    inputs = INPUT_COUNT // sources
    group = LANES // inputs
    half = planes // 2
    eighth = planes // 4
    frames = lanes // inputs
    step = pl.program_id(0)

    @pl.when(step == 0)
    def _():
        out_ref[...] = past_ref[...]

    for block in range(lanes // LANES):
        for lead in range(0, sources, group):
            tiles = [z_ref[lead + s, :, block * LANES : (block + 1) * LANES] for s in range(group)]
            for t in range(group):
                joined = jnp.concatenate([tile[:, t * inputs : (t + 1) * inputs] for tile in tiles], axis=1)
                at = (block * group + t) * planes
                rows_ref[at : at + planes, lead * inputs : lead * inputs + LANES] = joined

    index = lax.broadcasted_iota(jnp.int32, (INPUT_COUNT, BASE_TILE), 0)

    def tile(k, carry):
        at = pl.ds(pl.multiple_of(k * BASE_TILE, BASE_TILE), BASE_TILE)
        first, second = (
            jnp.dot(
                rows_ref[...],
                jnp.where(index == pairs_ref[row : row + 1, at], 1.0, 0.0).astype(jnp.bfloat16),
                preferred_element_type=jnp.float32,
            )
            for row in range(2)
        )
        first = first.reshape(frames, 2, 2, eighth, BASE_TILE)
        second = second.reshape(frames, 2, 2, eighth, BASE_TILE)
        real = jnp.sum(first[:, :, 0] * second[:, :, 0] + first[:, :, 1] * second[:, :, 1], axis=0)
        imag = jnp.sum(first[:, :, 1] * second[:, :, 0] - first[:, :, 0] * second[:, :, 1], axis=0)
        for parity in range(2):
            base = parity * half
            out_ref[base : base + eighth, at] += real[parity]
            out_ref[base + eighth : base + half, at] += imag[parity]
        return carry

    lax.fori_loop(0, pairs_ref.shape[1] // BASE_TILE, tile, 0, unroll=UNROLL)


def correlate(received, pairs, past):
    sources, planes, lanes = received.shape
    inputs = INPUT_COUNT // sources
    frames = lanes // inputs
    per_step = max(f for f in range(4, CORR_STEP + 1, 4) if frames % f == 0)
    count = pairs.shape[1]
    whole = lambda a: pl.BlockSpec(a.shape, lambda j: (0, 0))
    return pl.pallas_call(
        corr_kernel,
        grid=(frames // per_step,),
        in_specs=[
            pl.BlockSpec((sources, planes, per_step * inputs), lambda j: (0, 0, j)),
            whole(pairs),
            whole(past),
        ],
        out_specs=whole(past),
        out_shape=jax.ShapeDtypeStruct(past.shape, jnp.float32),
        scratch_shapes=[pltpu.VMEM((per_step * planes, INPUT_COUNT), jnp.bfloat16)],
        compiler_params=pltpu.CompilerParams(vmem_limit_bytes=CORR_GRANT),
        cost_estimate=pl.CostEstimate(
            flops=4 * frames * planes * INPUT_COUNT * count,
            bytes_accessed=2 * sources * planes * lanes,
            transcendentals=0,
        ),
        name="corr",
    )(received, pairs, past)


def power_kernel(table_ref, values_ref, out_ref):
    delays = jnp.dot(table_ref[...], values_ref[...], preferred_element_type=jnp.float32)
    out_ref[...] = delays[:CHANNEL_COUNT] ** 2 + delays[CHANNEL_COUNT:] ** 2


def delay_power(table, values):
    return pl.pallas_call(
        power_kernel,
        out_shape=jax.ShapeDtypeStruct((CHANNEL_COUNT, values.shape[1]), jnp.float32),
        compiler_params=pltpu.CompilerParams(vmem_limit_bytes=POWER_GRANT),
        name="power",
    )(table, values)


def prototype_table():
    count = TAPS * NFFT
    positions = jnp.arange(count, dtype=jnp.float32)
    start_shift = (positions - count / 2 + 0.5) / NFFT
    hamming = 0.54 - 0.46 * jnp.cos(2 * jnp.pi * positions / (count - 1))
    return (jnp.sinc(start_shift) * hamming).reshape(TAPS, NFFT)


def plain_filter_bank(voltages, antenna_flags, first_input, count):
    framed = voltages.astype(jnp.float32).reshape(voltages.shape[0], -1, NFFT)
    prototype = prototype_table()
    filtered = jnp.zeros((voltages.shape[0], count, NFFT), jnp.float32)
    for tap_index in range(TAPS):
        filtered = (
            filtered
            + prototype[tap_index][None, None, :]
            * framed[:, first_input + tap_index : first_input + tap_index + count, :]
        )
    return filtered * antenna_flags.astype(jnp.float32)[:, None, None]


def transform_table():
    rows_int = jnp.arange(2 * CHANNEL_COUNT, dtype=jnp.int32)
    channel = rows_int // 2
    is_real = rows_int % 2 == 0
    sample = jnp.arange(NFFT, dtype=jnp.int32)
    phase = channel[:, None] * sample[None, :] % NFFT
    angle = 2 * jnp.pi * phase.astype(jnp.float32) / NFFT
    table = jnp.where(is_real[:, None], jnp.cos(angle), -jnp.sin(angle))
    return table / math.sqrt(NFFT)


def delay_table():
    chan_int = jnp.arange(CHANNEL_COUNT, dtype=jnp.int32)
    chan_float = chan_int.astype(jnp.float32)
    base = 2 * jnp.pi * chan_float / (CHANNEL_COUNT - 1)
    window = (
        0.35875
        - 0.48829 * jnp.cos(base)
        + 0.14128 * jnp.cos(2 * base)
        - 0.01168 * jnp.cos(3 * base)
    )
    phase = chan_int[:, None] * chan_int[None, :] % CHANNEL_COUNT
    angle = 2 * jnp.pi * phase.astype(jnp.float32) / CHANNEL_COUNT
    cosine = jnp.cos(angle) * window[None, :]
    sine = jnp.sin(angle) * window[None, :]
    upper = jnp.concatenate([cosine, sine], axis=1)
    lower = jnp.concatenate([-sine, cosine], axis=1)
    table = jnp.concatenate([upper, lower], axis=0) / jnp.sqrt(jnp.sum(window * window))
    return table.astype(jnp.bfloat16)


def plain_correlate(received):
    values = received[0]
    swapped = jnp.stack([values[:, 1], -values[:, 0]], axis=1)
    stacked = jnp.stack([values, swapped], axis=0)
    return jnp.einsum("qcrit,crjt->iqcj", stacked, values, preferred_element_type=jnp.float32)


def plain_device(voltages, antenna_flags, baseline_pairs):
    width = lax.axis_size("wide")
    local_inputs = voltages.shape[0]
    local_channels = CHANNEL_COUNT // width
    table = transform_table()
    scale = 1.0 / math.sqrt(2 * NT)
    correlation = jnp.zeros((INPUT_COUNT, 2, local_channels, INPUT_COUNT), jnp.float32)
    for batch_index in range(2):
        filtered = plain_filter_bank(voltages, antenna_flags, batch_index * NT, NT)
        raw = jnp.einsum(
            "kn,itn->kit",
            table,
            filtered,
            precision=lax.Precision.HIGHEST,
            preferred_element_type=jnp.float32,
        )
        correlation = correlation + plain_correlate(
            lax.all_to_all(
                raw.astype(jnp.bfloat16).reshape(width, local_channels, 2, local_inputs, NT),
                "wide",
                split_axis=0,
                concat_axis=3,
                tiled=True,
            )
        )
    baseline_count = baseline_pairs.shape[1]
    block_size = math.gcd(baseline_count, 1024)
    first_blocks = baseline_pairs[0].reshape(baseline_count // block_size, block_size)
    second_blocks = baseline_pairs[1].reshape(baseline_count // block_size, block_size)
    input_positions = jnp.arange(INPUT_COUNT, dtype=jnp.int32)

    def select_block(indices):
        first_block, second_block = indices
        rows_taken = jnp.take(correlation, first_block, axis=0)
        selector = (input_positions[None, :] == second_block[:, None]).astype(jnp.float32)
        return jnp.sum(rows_taken * selector[:, None, None, :], axis=3)

    selected = lax.map(select_block, (first_blocks, second_blocks))
    selected = selected.reshape(baseline_count, 2, local_channels)
    picked = (jnp.transpose(selected, (1, 2, 0)) * scale).astype(jnp.bfloat16)
    regrouped = lax.all_to_all(picked, "wide", split_axis=2, concat_axis=1, tiled=True)
    column_list = regrouped.reshape(2 * CHANNEL_COUNT, regrouped.shape[2])
    delays = jnp.dot(delay_table(), column_list, preferred_element_type=jnp.float32)
    return delays[:CHANNEL_COUNT] ** 2 + delays[CHANNEL_COUNT:] ** 2


def tiles(local_inputs, local_channels, count, width):
    fits = local_inputs % 16 == 0 and LANES % local_inputs == 0 and local_channels % 16 == 0
    return fits and count % BASE_TILE == 0 and (count // width) % LANES == 0


def per_device(voltages, antenna_flags, baseline_pairs):
    width = lax.axis_size("wide")
    local_inputs = voltages.shape[0]
    local_channels = CHANNEL_COUNT // width
    planes = 2 * local_channels
    count = baseline_pairs.shape[1]
    if not tiles(local_inputs, local_channels, count, width):
        return plain_device(voltages, antenna_flags, baseline_pairs)
    proto = jnp.asarray(prototype_np())
    even, odd = (jnp.asarray(transform_np(parity, width)) for parity in range(2))
    flags = antenna_flags[None, :]
    total = jnp.zeros((planes, count), jnp.float32)
    waiting = []
    start = 0
    for frames in CHUNKS:
        spectra = filter_bank(voltages, proto, flags, even, odd, start, frames, width)
        if len(waiting) > 1:
            total = correlate(waiting.pop(0), baseline_pairs, total)
            spectra, total = lax.optimization_barrier((spectra, total))
        waiting.append(lax.all_to_all(spectra, "wide", split_axis=0, concat_axis=0, tiled=True))
        start += frames
    for received in waiting:
        total = correlate(received, baseline_pairs, total)
    picked = (total * (1.0 / math.sqrt(FRAMES))).astype(jnp.bfloat16)
    picked = picked.reshape(planes, width, count // width).transpose(1, 0, 2)
    regrouped = lax.all_to_all(picked, "wide", split_axis=0, concat_axis=0, tiled=True)
    return delay_power(jnp.asarray(delay_np(width)), regrouped.reshape(2 * CHANNEL_COUNT, count // width))


def solution(mesh):
    placed = (P("wide", "groups"), P(("groups", "wide")), P())
    return jax.shard_map(
        per_device, mesh=mesh, in_specs=placed, out_specs=P("groups", "wide"), check_vma=False
    )
```
